32 devices in a mesh: dp: 8 (over y, x, core), tensor: 4 (over z).
Axes of the slice: x: 2, y: 2, z: 4, core: 2. Of those that a mesh axis runs over, the one named last changes fastest.
Arguments:
- tokens: bfloat16 [4096, 1536], P('dp'), may hold values from -6 to 6
- cotangent: bfloat16 [4096, 1536], P('dp'), may hold values from -6 to 6
- lengths: int32 [8, 4], P('dp'), may hold values from 1 to 256, 512 in all within a row
- gate_weight: float32 [1536, 3072], P('dp', 'tensor'), may hold values from -0.15625 to 0.15625
- inner_weight: float32 [1536, 3072], P('dp', 'tensor'), may hold values from -0.15625 to 0.15625
- output_weight: float32 [1536, 3072], P('dp', 'tensor'), may hold values from -0.109375 to 0.109375
- delta_weight: float32 [1536, 48], P('dp', 'tensor'), may hold values from -0.15625 to 0.15625
- state_weight: float32 [1536, 256], P('dp'), may hold values from -0.15625 to 0.15625
- inner_filter: float32 [5, 3072], P(None, 'tensor'), may hold values from -0.5 to 0.5
- state_filter: float32 [5, 256], replicated, may hold values from -0.5 to 0.5
- head_scalars: float32 [3, 48], P(None, 'tensor'), may hold values from -7 to 2, as said below
- norm_gain: float32 [3072], P('tensor'), may hold values from 0.5 to 1.5
- input_gain: float32 [1536], replicated, may hold values from 0.5 to 1.5
- gate_moment: float32 [1536, 3072], P('dp', 'tensor'), may hold values from -64 to 64
- inner_moment: float32 [1536, 3072], P('dp', 'tensor'), may hold values from -64 to 64
- output_moment: float32 [1536, 3072], P('dp', 'tensor'), may hold values from -64 to 64
- delta_moment: float32 [1536, 48], P('dp', 'tensor'), may hold values from -32 to 32
- state_moment: float32 [1536, 256], P('dp'), may hold values from -32 to 32
- inner_filter_moment: float32 [5, 3072], P(None, 'tensor'), may hold values from -64 to 64
- state_filter_moment: float32 [5, 256], replicated, may hold values from -64 to 64
- head_scalars_moment: float32 [3, 48], P(None, 'tensor'), may hold values from -64 to 64
- norm_gain_moment: float32 [3072], P('tensor'), may hold values from -64 to 64
- input_gain_moment: float32 [1536], replicated, may hold values from -64 to 64
Outputs:
- block_output: bfloat16 [4096, 1536], P('dp')
- input_gradient: float32 [4096, 1536], P('dp')
- gate_gradient: float32 [1536, 3072], P('dp', 'tensor')
- inner_gradient: float32 [1536, 3072], P('dp', 'tensor')
- output_gradient: float32 [1536, 3072], P('dp', 'tensor')
- delta_gradient: float32 [1536, 48], P('dp', 'tensor')
- state_gradient: float32 [1536, 256], P('dp')
- inner_filter_gradient: float32 [5, 3072], P(None, 'tensor')
- state_filter_gradient: float32 [5, 256], replicated
- head_scalars_gradient: float32 [3, 48], P(None, 'tensor')
- norm_gain_gradient: float32 [3072], P('tensor')
- input_gain_gradient: float32 [1536], replicated
- gate_updated: float32 [1536, 3072], P('dp', 'tensor')
- inner_updated: float32 [1536, 3072], P('dp', 'tensor')
- output_updated: float32 [1536, 3072], P('dp', 'tensor')
- delta_updated: float32 [1536, 48], P('dp', 'tensor')
- state_updated: float32 [1536, 256], P('dp')
- inner_filter_updated: float32 [5, 3072], P(None, 'tensor')
- state_filter_updated: float32 [5, 256], replicated
- head_scalars_updated: float32 [3, 48], P(None, 'tensor')
- norm_gain_updated: float32 [3072], P('tensor')
- input_gain_updated: float32 [1536], replicated
- gate_moment_new: float32 [1536, 3072], P('dp', 'tensor')
- inner_moment_new: float32 [1536, 3072], P('dp', 'tensor')
- output_moment_new: float32 [1536, 3072], P('dp', 'tensor')
- delta_moment_new: float32 [1536, 48], P('dp', 'tensor')
- state_moment_new: float32 [1536, 256], P('dp')
- inner_filter_moment_new: float32 [5, 3072], P(None, 'tensor')
- state_filter_moment_new: float32 [5, 256], replicated
- head_scalars_moment_new: float32 [3, 48], P(None, 'tensor')
- norm_gain_moment_new: float32 [3072], P('tensor')
- input_gain_moment_new: float32 [1536], replicated
The draws below stay inside these ranges and needn't reach their ends.
Inputs may be any that keep to these rules, and one draw needn't show every extreme that they name: Each row holds the lengths of the 4 sequences packed in order into one device's 512 tokens; they sum to 512 and the largest is exactly 256. `head_scalars`: row 0 holds offsets of the step sizes, row 1 logarithms of decay rates, row 2 skip weights.
All inputs are finite; a program needn't handle non-finite values.
Results may differ from the reference program's by a relative error of at most 0.008.
The reference program's roundings to bfloat16 on the way (of `normed`, `normalized` and `grad_projected`) count: a program that leaves them out, or rounds other values in their place, can miss the bound.
Values may be sent and summed in bfloat16 or wider, within the bound.
No kernel may reach another device: no remote copies, remote signals or barrier semaphores. Data moves between devices by JAX's collectives and lax.ppermute only.
A program may use at most 192 MiB of HBM per device.

```python
import math
import jax
import jax.numpy as jnp
import numpy as np
from jax import lax

D = 1536
INNER = 3072
HEADS = 48
NSTATE = 128
CONV = 4
SPAN = 256
SCHULZ = 5
SEQ_DEV = 4
TOK_DEV = 512
MAXLEN = 256
TOKENS = 4096
N_DP = 8


def draw_head_scalars(key, part):
    first_key = jax.random.fold_in(key, 11)
    second_key = jax.random.fold_in(key, 23)
    third_key = jax.random.fold_in(key, 37)
    offsets = jax.random.uniform(first_key, (HEADS,), jnp.float32, -6.0, -2.0)
    decay_logs = jax.random.uniform(second_key, (HEADS,), jnp.float32, -1.0, 1.5)
    skips = jax.random.uniform(third_key, (HEADS,), jnp.float32, 0.5, 1.5)
    return jnp.stack([offsets, decay_logs, skips])


def level_of(key, extent, shards, smallest, high):
    def one(dim, shards_of):
        heights = jax.random.uniform(jax.random.fold_in(jax.random.fold_in(key, 6), dim), (shards_of,), jnp.float32, smallest / len(shards), high / len(shards))
        return jnp.repeat(jnp.exp(heights), extent[dim] // shards_of).reshape((-1,) + (1,) * (len(extent) - dim - 1))

    loudness = one(*shards[0])
    for cut in shards[1:]:
        loudness = loudness * one(*cut)
    return loudness


def split_up(count, total, bound, skew):
    loads = [(1 << 20) // math.isqrt(grade ** skew) + 1 for grade in range(2, count + 1)]
    rest, holding = total - bound - (count - 1), [1] * (count - 1)
    while rest > 0:
        movable = [i for i in range(count - 1) if holding[i] < bound]
        mass, left = sum([loads[i] for i in movable]), rest
        for i in movable:
            addition = min(bound - holding[i], max(1, left * loads[i] // mass), rest)
            holding[i] = holding[i] + addition
            rest = rest - addition
    return np.array([bound] + holding)


def uneven(own_key, number_of, total, most, lean):
    if number_of == 2:
        one = jax.random.randint(own_key, (), max(1, total - most), min(most, total - 1) + 1)
        return jnp.stack([one, total - one])
    sizes = jnp.asarray(split_up(number_of, total, most, lean), jnp.int32)
    pairs = (number_of - 1) // 2
    source_of, receiver = sizes[1:1 + 2 * pairs:2], sizes[2:2 + 2 * pairs:2]
    room = jnp.minimum(source_of - 1, most - receiver)
    moved = jax.random.randint(jax.random.fold_in(own_key, 1), (pairs,), 0, 1 << 20) % (room + 1)
    sizes = sizes.at[1:1 + 2 * pairs:2].set(source_of - moved).at[2:2 + 2 * pairs:2].set(receiver + moved)
    return sizes[jax.random.permutation(jax.random.fold_in(own_key, 2), number_of)]


def centred(stream_key, extent, scale, limit, cuts=(), held_as=jnp.bfloat16):
    result = scale * jax.random.normal(stream_key, extent, jnp.float32)
    if cuts:
        result = result * level_of(stream_key, extent, cuts, -0.22, 0.18)
    return jnp.clip(result, -limit, limit).astype(held_as)


def setup_inputs(seed: int = 0) -> dict:
    arg_keys = jax.random.split(jax.random.key(seed), 24)
    return {
        "tokens": centred(arg_keys[0], (TOKENS, D), 1.0, 6.0, ((0, 8),)),
        "cotangent": centred(arg_keys[1], (TOKENS, D), 1.0, 6.0, ((0, 8),)),
        "lengths": jax.vmap(lambda own: uneven(own, SEQ_DEV, TOK_DEV, MAXLEN, 2))(jax.random.split(arg_keys[2], N_DP)).reshape((N_DP, SEQ_DEV)).astype(jnp.int32),
        "gate_weight": centred(arg_keys[3], (D, INNER), D ** -0.5, 0.15625, ((0, 8), (1, 4)), jnp.float32),
        "inner_weight": centred(arg_keys[4], (D, INNER), D ** -0.5, 0.15625, ((0, 8), (1, 4)), jnp.float32),
        "output_weight": centred(arg_keys[5], (D, INNER), INNER ** -0.5, 0.109375, ((0, 8), (1, 4)), jnp.float32),
        "delta_weight": centred(arg_keys[6], (D, HEADS), D ** -0.5, 0.15625, ((0, 8), (1, 4)), jnp.float32),
        "state_weight": centred(arg_keys[7], (D, 2 * NSTATE), D ** -0.5, 0.15625, ((0, 8),), jnp.float32),
        "inner_filter": jnp.clip(jax.random.uniform(arg_keys[8], (CONV + 1, INNER), jnp.float32, -0.5, 0.5) * level_of(arg_keys[8], (CONV + 1, INNER), ((1, 4),), -0.4, 0.0), -0.5, 0.5),
        "state_filter": jnp.clip(jax.random.uniform(arg_keys[9], (CONV + 1, 2 * NSTATE), jnp.float32, -0.5, 0.5), -0.5, 0.5),
        "head_scalars": draw_head_scalars(jax.random.fold_in(arg_keys[23], 71), 0),
        "norm_gain": jnp.clip(1.0 + 0.1 * jax.random.normal(arg_keys[11], (INNER,), jnp.float32), 0.5, 1.5),
        "input_gain": jnp.clip(1.0 + 0.1 * jax.random.normal(arg_keys[12], (D,), jnp.float32), 0.5, 1.5),
        "gate_moment": centred(arg_keys[13], (D, INNER), (TOK_DEV * N_DP // 1024 + 8), 64.0, ((0, 8), (1, 4)), jnp.float32),
        "inner_moment": centred(arg_keys[14], (D, INNER), (TOK_DEV * N_DP // 1024 + 8), 64.0, ((0, 8), (1, 4)), jnp.float32),
        "output_moment": centred(arg_keys[15], (D, INNER), (TOK_DEV * N_DP // 1024 + 8), 64.0, ((0, 8), (1, 4)), jnp.float32),
        "delta_moment": centred(arg_keys[16], (D, HEADS), (TOK_DEV * N_DP // 2048 + 4), 32.0, ((0, 8), (1, 4)), jnp.float32),
        "state_moment": centred(arg_keys[17], (D, 2 * NSTATE), (TOK_DEV * N_DP // 2048 + 4), 32.0, ((0, 8),), jnp.float32),
        "inner_filter_moment": centred(arg_keys[18], (CONV + 1, INNER), (TOK_DEV * N_DP // 1024 + 8), 64.0, ((1, 4),), jnp.float32),
        "state_filter_moment": centred(arg_keys[19], (CONV + 1, 2 * NSTATE), (TOK_DEV * N_DP // 1024 + 8), 64.0, (), jnp.float32),
        "head_scalars_moment": centred(arg_keys[20], (3, HEADS), (TOK_DEV * N_DP // 1024 + 8), 64.0, ((1, 4),), jnp.float32),
        "norm_gain_moment": centred(arg_keys[21], (INNER,), (TOK_DEV * N_DP // 1024 + 8), 64.0, ((0, 4),), jnp.float32),
        "input_gain_moment": centred(arg_keys[22], (D,), (TOK_DEV * N_DP // 1024 + 8), 64.0, (), jnp.float32),
    }


norm_epsilon = 1e-05
moment_decay = 0.95
muon_rate = 0.02
plain_rate = 0.002
schulz_terms = (3.4445, -4.775, 2.0315)
exact_mode = lax.Precision.HIGHEST

def packing_layout(length_row, row_count):
    ends = jnp.cumsum(length_row).astype(jnp.int32)
    places = jnp.arange(row_count, dtype=jnp.int32)
    after = (places[:, None] >= ends[None, :]).astype(jnp.int32)
    segment = lax.optimization_barrier(jnp.sum(after, axis=1)).astype(jnp.int32)
    starts = lax.optimization_barrier(jnp.sum(after * length_row[None, :], axis=1)).astype(jnp.int32)
    return (segment, places - starts)

def shifted_rows(values, offset):
    padding = jnp.zeros((offset, values.shape[1]), values.dtype)
    return jnp.concatenate([padding, values[:values.shape[0] - offset]], axis=0)

def causal_filter(values, taps, position):
    summed = taps[CONV] + taps[CONV - 1] * values
    for offset in range(1, CONV):
        inside = (position >= offset).astype(jnp.float32)[:, None]
        summed = summed + taps[CONV - 1 - offset] * shifted_rows(values, offset) * inside
    return jax.nn.silu(summed)

def state_mixer(gate_part, inner_part, delta_raw, entry_rows, readout_rows, inner_filter, head_scalars, segment, position):
    row_count, head_count = delta_raw.shape
    head_width = inner_part.shape[1] // head_count
    block_count = row_count // SPAN
    filtered = causal_filter(inner_part, inner_filter, position)
    delta_step = jax.nn.softplus(delta_raw + head_scalars[0])
    step_log = delta_step * -jnp.exp(head_scalars[1])
    heads_in = filtered.reshape(row_count, head_count, head_width)
    driven = (heads_in * delta_step[:, :, None]).reshape(block_count, SPAN, head_count, head_width)
    lower_mask = (jnp.arange(SPAN)[:, None] >= jnp.arange(SPAN)[None, :]).astype(jnp.float32)
    running = jnp.einsum('ij,cjh->cih', lower_mask, step_log.reshape(block_count, SPAN, head_count), precision=exact_mode)
    block_seg = segment.reshape(block_count, SPAN)
    same_seq = (block_seg[:, :, None] == block_seg[:, None, :]).astype(jnp.float32) * lower_mask
    spread = running[:, :, None, :] - running[:, None, :, :]
    entry_blocks = entry_rows.reshape(block_count, SPAN, -1)
    readout_blocks = readout_rows.reshape(block_count, SPAN, -1)
    correlation = jnp.einsum('cin,cjn->cij', readout_blocks, entry_blocks, precision=exact_mode)
    mixing = jnp.exp(jnp.minimum(spread, 0.0)) * (correlation * same_seq)[:, :, :, None]
    within = jnp.einsum('cijh,cjhp->cihp', mixing, driven, precision=exact_mode)
    final_log = running[:, -1, :]
    last_seg = block_seg[:, -1]
    tail_weight = jnp.exp(final_log[:, None, :] - running) * (block_seg == last_seg[:, None]).astype(jnp.float32)[:, :, None]
    fresh_states = jnp.einsum('cjh,cjhp,cjn->chpn', tail_weight, driven, entry_blocks, precision=exact_mode)
    prior_seg = jnp.concatenate([jnp.full((1,), -1, dtype=jnp.int32), last_seg[:-1]])
    carry_keep = (last_seg == prior_seg).astype(jnp.float32)

    def advance(carried_state, pieces):
        keep_flag, total_log, update = pieces
        return (keep_flag * jnp.exp(total_log)[:, None, None] * carried_state + update, carried_state)
    start_state = jnp.zeros(fresh_states.shape[1:], jnp.float32)
    final_state, entering = lax.scan(advance, start_state, (carry_keep, final_log, fresh_states))
    reach_weight = jnp.exp(running) * (block_seg == prior_seg[:, None]).astype(jnp.float32)[:, :, None]
    carried = jnp.einsum('cih,cin,chpn->cihp', reach_weight, readout_blocks, entering, precision=exact_mode)
    outputs = (within + carried).reshape(row_count, head_count, head_width) + head_scalars[2][None, :, None] * heads_in
    return outputs.reshape(row_count, head_count * head_width) * jax.nn.silu(gate_part)

def newton_schulz(rounded):
    widened = rounded.astype(jnp.float32)
    frobenius = jnp.sqrt(jnp.sum(widened * widened))
    iterate = (widened / (frobenius + 1e-07)).astype(jnp.bfloat16)
    for sweep in range(SCHULZ):
        gram_matrix = jnp.dot(iterate, iterate.T, preferred_element_type=jnp.float32)
        gram_low = gram_matrix.astype(jnp.bfloat16)
        squared = jnp.dot(gram_low, gram_low, preferred_element_type=jnp.float32)
        polynomial = (schulz_terms[1] * gram_matrix + schulz_terms[2] * squared).astype(jnp.bfloat16)
        iterate = (schulz_terms[0] * iterate.astype(jnp.float32) + jnp.dot(polynomial, iterate, preferred_element_type=jnp.float32)).astype(jnp.bfloat16)
    return iterate

def block_pass(tokens_rows, upstream, length_row, in_matrix, out_matrix, inner_filter, state_filter, head_scalars, norm_gain, input_gain):
    row_count = tokens_rows.shape[0]
    segment, position = packing_layout(length_row, row_count)
    tokens_wide = tokens_rows.astype(jnp.float32)
    root_scale = lax.rsqrt(lax.optimization_barrier(jnp.mean(tokens_wide * tokens_wide, axis=1, keepdims=True)) + norm_epsilon)
    normed = (tokens_wide * root_scale * input_gain).astype(jnp.bfloat16)
    projected = jnp.dot(normed, in_matrix, preferred_element_type=jnp.float32)
    mixing_cols = 2 * INNER + HEADS
    gate_part = projected[:, :INNER]
    inner_part = projected[:, INNER:2 * INNER]
    delta_raw = projected[:, 2 * INNER:mixing_cols]
    state_raw = projected[:, mixing_cols:]

    def state_rows(raw_values, taps):
        filtered = causal_filter(raw_values, taps, position)
        return (filtered[:, :NSTATE], filtered[:, NSTATE:])

    def mixer(gate_in, inner_in, delta_in, entry_in, readout_in, taps, scalars):
        return state_mixer(gate_in, inner_in, delta_in, entry_in, readout_in, taps, scalars, segment, position)
    (entry_rows, readout_rows), state_back = jax.vjp(state_rows, state_raw, state_filter)
    gated, mixer_back = jax.vjp(mixer, gate_part, inner_part, delta_raw, entry_rows, readout_rows, inner_filter, head_scalars)
    norm_scale = lax.rsqrt(lax.optimization_barrier(jnp.mean(gated * gated, axis=1, keepdims=True)) + norm_epsilon)
    normalized = (gated * norm_scale * norm_gain).astype(jnp.bfloat16)
    block_out = (tokens_wide + jnp.dot(normalized, out_matrix.T, preferred_element_type=jnp.float32)).astype(jnp.bfloat16)
    grad_normalized = jnp.dot(upstream, out_matrix, preferred_element_type=jnp.float32)
    out_grad = jnp.dot(upstream.T, normalized, preferred_element_type=jnp.float32)
    norm_gain_grad = lax.optimization_barrier(jnp.sum(grad_normalized * gated * norm_scale, axis=0))
    weighted = grad_normalized * norm_gain
    grad_gated = norm_scale * weighted - gated * norm_scale ** 3 * lax.optimization_barrier(jnp.mean(weighted * gated, axis=1, keepdims=True))
    grad_gate, grad_inner, grad_delta, grad_entry, grad_readout, filter_grad, scalar_grad = mixer_back(grad_gated)
    grad_state, state_filter_grad = state_back((grad_entry, grad_readout))
    grad_projected = jnp.concatenate([grad_gate, grad_inner, grad_delta, grad_state], axis=1).astype(jnp.bfloat16)
    grad_normed = jnp.dot(grad_projected, in_matrix.T, preferred_element_type=jnp.float32)
    in_grad = jnp.dot(normed.T, grad_projected, preferred_element_type=jnp.float32)
    input_gain_grad = lax.optimization_barrier(jnp.sum(grad_normed * tokens_wide * root_scale, axis=0))
    weighted_in = grad_normed * input_gain
    input_grad = upstream.astype(jnp.float32) + root_scale * weighted_in - tokens_wide * root_scale ** 3 * lax.optimization_barrier(jnp.mean(weighted_in * tokens_wide, axis=1, keepdims=True))
    return (block_out, input_grad, (in_grad, out_grad, filter_grad, state_filter_grad, scalar_grad, norm_gain_grad, input_gain_grad))

def muon_update(weight, moment, gradient):
    fresh = moment_decay * moment + gradient
    factor = 0.2 * math.sqrt(max(D, INNER))
    ortho = newton_schulz(fresh.astype(jnp.bfloat16)).astype(jnp.float32)
    return (weight - muon_rate * factor * ortho, fresh)

def plain_update(weight, moment, gradient):
    fresh = moment_decay * moment + gradient
    return (weight - plain_rate * fresh, fresh)

def reference(tokens, cotangent, lengths, gate_weight, inner_weight, output_weight, delta_weight, state_weight, inner_filter, state_filter, head_scalars, norm_gain, input_gain, gate_moment, inner_moment, output_moment, delta_moment, state_moment, inner_filter_moment, state_filter_moment, head_scalars_moment, norm_gain_moment, input_gain_moment):
    in_matrix = jnp.concatenate([gate_weight, inner_weight, delta_weight, state_weight], axis=1).astype(jnp.bfloat16)
    out_matrix = output_weight.astype(jnp.bfloat16)

    def one_block(totals, pieces):
        tokens_rows, upstream, length_row = pieces
        block_out, input_grad, grads = block_pass(tokens_rows, upstream, length_row, in_matrix, out_matrix, inner_filter, state_filter, head_scalars, norm_gain, input_gain)
        return (jax.tree.map(jnp.add, totals, grads), (block_out, input_grad))
    initial = (jnp.zeros((D, 2 * INNER + HEADS + 2 * NSTATE), jnp.float32), jnp.zeros((D, INNER), jnp.float32), jnp.zeros((CONV + 1, INNER), jnp.float32), jnp.zeros((CONV + 1, 2 * NSTATE), jnp.float32), jnp.zeros((3, HEADS), jnp.float32), jnp.zeros((INNER,), jnp.float32), jnp.zeros((D,), jnp.float32))
    totals, (block_outs, input_grads) = lax.scan(one_block, initial, (tokens.reshape(N_DP, TOK_DEV, D), cotangent.reshape(N_DP, TOK_DEV, D), lengths))
    in_grad, output_gradient, inner_filter_gradient, state_filter_gradient, head_scalars_gradient, norm_gain_gradient, input_gain_gradient = totals
    gate_gradient = in_grad[:, :INNER]
    inner_gradient = in_grad[:, INNER:2 * INNER]
    delta_gradient = in_grad[:, 2 * INNER:2 * INNER + HEADS]
    state_gradient = in_grad[:, 2 * INNER + HEADS:]
    gate_updated, gate_moment_new = muon_update(gate_weight, gate_moment, gate_gradient)
    inner_updated, inner_moment_new = muon_update(inner_weight, inner_moment, inner_gradient)
    output_updated, output_moment_new = muon_update(output_weight, output_moment, output_gradient)
    delta_updated, delta_moment_new = plain_update(delta_weight, delta_moment, delta_gradient)
    state_updated, state_moment_new = plain_update(state_weight, state_moment, state_gradient)
    inner_filter_updated, inner_filter_moment_new = plain_update(inner_filter, inner_filter_moment, inner_filter_gradient)
    state_filter_updated, state_filter_moment_new = plain_update(state_filter, state_filter_moment, state_filter_gradient)
    head_scalars_updated, head_scalars_moment_new = plain_update(head_scalars, head_scalars_moment, head_scalars_gradient)
    norm_gain_updated, norm_gain_moment_new = plain_update(norm_gain, norm_gain_moment, norm_gain_gradient)
    input_gain_updated, input_gain_moment_new = plain_update(input_gain, input_gain_moment, input_gain_gradient)
    return (block_outs.reshape(TOKENS, D), input_grads.reshape(TOKENS, D), gate_gradient, inner_gradient, output_gradient, delta_gradient, state_gradient, inner_filter_gradient, state_filter_gradient, head_scalars_gradient, norm_gain_gradient, input_gain_gradient, gate_updated, inner_updated, output_updated, delta_updated, state_updated, inner_filter_updated, state_filter_updated, head_scalars_updated, norm_gain_updated, input_gain_updated, gate_moment_new, inner_moment_new, output_moment_new, delta_moment_new, state_moment_new, inner_filter_moment_new, state_filter_moment_new, head_scalars_moment_new, norm_gain_moment_new, input_gain_moment_new)
```

```python
import math

import jax
import jax.numpy as jnp
from jax import lax
from jax.experimental import pallas as pl
from jax.experimental.pallas import tpu as pltpu
from jax.sharding import PartitionSpec as P

D = 1536
INNER = 3072
NSTATE = 128
CONV = 4
SPAN = 256
SCHULZ = 5
GROUP = 3
TILE = 256
SLAB = 512


norm_epsilon = 1e-05
moment_decay = 0.95
muon_rate = 0.02
plain_rate = 0.002
schulz_terms = (3.4445, -4.775, 2.0315)
exact_mode = lax.Precision.HIGHEST


def packing_layout(length_row, row_count):
    ends = jnp.cumsum(length_row)
    places = jnp.arange(row_count, dtype=jnp.int32)
    after = (places[:, None] >= ends[None, :]).astype(jnp.int32)
    segment = jnp.sum(after, axis=1)
    starts = jnp.sum(after * length_row[None, :], axis=1)
    return (segment, places - starts)


def shifted_rows(values, offset):
    padding = jnp.zeros((offset, values.shape[1]), values.dtype)
    return jnp.concatenate([padding, values[: values.shape[0] - offset]], axis=0)


def causal_filter(values, taps, position):
    summed = taps[CONV] + taps[CONV - 1] * values
    for offset in range(1, CONV):
        inside = (position >= offset).astype(jnp.float32)[:, None]
        summed = summed + taps[CONV - 1 - offset] * shifted_rows(values, offset) * inside
    return jax.nn.silu(summed)


def state_mixer(
    gate_part,
    inner_part,
    delta_raw,
    entry_rows,
    readout_rows,
    inner_filter,
    head_scalars,
    segment,
    position,
):
    row_count, head_count = delta_raw.shape
    head_width = inner_part.shape[1] // head_count
    block_count = row_count // SPAN
    filtered = causal_filter(inner_part, inner_filter, position)
    delta_step = jax.nn.softplus(delta_raw + head_scalars[0])
    step_log = delta_step * -jnp.exp(head_scalars[1])
    heads_in = filtered.reshape(row_count, head_count, head_width)
    driven = (heads_in * delta_step[:, :, None]).reshape(block_count, SPAN, head_count, head_width)
    lower_mask = (jnp.arange(SPAN)[:, None] >= jnp.arange(SPAN)[None, :]).astype(jnp.float32)
    running = jnp.einsum(
        "ij,cjh->cih",
        lower_mask,
        step_log.reshape(block_count, SPAN, head_count),
        precision=exact_mode,
    )
    block_seg = segment.reshape(block_count, SPAN)
    same_seq = (block_seg[:, :, None] == block_seg[:, None, :]).astype(jnp.float32) * lower_mask
    spread = running[:, :, None, :] - running[:, None, :, :]
    entry_blocks = entry_rows.reshape(block_count, SPAN, -1)
    readout_blocks = readout_rows.reshape(block_count, SPAN, -1)
    correlation = jnp.einsum("cin,cjn->cij", readout_blocks, entry_blocks, precision=exact_mode)
    mixing = jnp.exp(jnp.minimum(spread, 0.0)) * (correlation * same_seq)[:, :, :, None]
    within = jnp.einsum("cijh,cjhp->cihp", mixing, driven, precision=exact_mode)
    final_log = running[:, -1, :]
    last_seg = block_seg[:, -1]
    tail_weight = (
        jnp.exp(final_log[:, None, :] - running)
        * (block_seg == last_seg[:, None]).astype(jnp.float32)[:, :, None]
    )
    fresh_states = jnp.einsum(
        "cjh,cjhp,cjn->chpn", tail_weight, driven, entry_blocks, precision=exact_mode
    )
    prior_seg = jnp.concatenate([jnp.full((1,), -1, dtype=jnp.int32), last_seg[:-1]])
    carry_keep = (last_seg == prior_seg).astype(jnp.float32)

    def advance(carried_state, pieces):
        keep_flag, total_log, update = pieces
        return (
            keep_flag * jnp.exp(total_log)[:, None, None] * carried_state + update,
            carried_state,
        )

    start_state = jnp.zeros(fresh_states.shape[1:], jnp.float32)
    final_state, entering = lax.scan(advance, start_state, (carry_keep, final_log, fresh_states))
    reach_weight = (
        jnp.exp(running) * (block_seg == prior_seg[:, None]).astype(jnp.float32)[:, :, None]
    )
    carried = jnp.einsum(
        "cih,cin,chpn->cihp", reach_weight, readout_blocks, entering, precision=exact_mode
    )
    outputs = (within + carried).reshape(row_count, head_count, head_width) + head_scalars[2][
        None, :, None
    ] * heads_in
    return outputs.reshape(row_count, head_count * head_width) * jax.nn.silu(gate_part)


def schulz_kernel(
    place, pieces, result, iterate, gram, mixed, low, poly, mixed_low, product, arrived
):
    holders, column_blocks, rows, columns = pieces.shape
    width = iterate.shape[0]
    blocks = width // TILE
    lead, slope, curve = schulz_terms

    def piece_copy(index):
        holder = index // column_blocks
        block = index % column_blocks
        return pltpu.make_async_copy(
            pieces.at[holder, block],
            iterate.at[
                pl.ds(pl.multiple_of(holder * rows, rows), rows),
                pl.ds(pl.multiple_of(block * columns, columns), columns),
            ],
            arrived.at[index],
        )

    def begin(index, carry):
        piece_copy(index).start()
        return carry

    def finish(index, carry):
        piece_copy(index).wait()
        return carry

    lax.fori_loop(0, holders * column_blocks, begin, 0)
    lax.fori_loop(0, holders * column_blocks, finish, 0)
    unit_rows = lax.broadcasted_iota(jnp.int32, (TILE, TILE), 0)
    unit_columns = lax.broadcasted_iota(jnp.int32, (TILE, TILE), 1)
    diagonal = unit_rows == unit_columns
    unit = jnp.where(diagonal, 1.0, 0.0).astype(jnp.bfloat16)

    def band(index):
        return slice(index * TILE, (index + 1) * TILE)

    def tail(index):
        return slice(index * TILE, width)

    def mirror(target):
        for upper in range(blocks):
            for right in range(upper + 1, blocks):
                flipped = lax.dot_general(
                    unit,
                    target[band(upper), band(right)],
                    (((1,), (1,)), ((), ())),
                    preferred_element_type=jnp.float32,
                )
                target[band(right), band(upper)] = flipped.astype(jnp.bfloat16)

    def half_product(left, right, finish_band):
        for index in range(blocks):
            finish_band(
                index,
                jnp.dot(
                    left[band(index), :],
                    right[:, tail(index)],
                    preferred_element_type=jnp.float32,
                ),
            )

    def sweep(step, carry):
        lead_power, shrink = carry
        opening = (step == 0) | (step == GROUP)

        @pl.when(opening)
        def _():
            for index in range(blocks):
                gram[band(index), tail(index)] = lax.dot_general(
                    iterate[band(index), :],
                    iterate[tail(index), :],
                    (((1,), (1,)), ((), ())),
                    preferred_element_type=jnp.float32,
                )

        trace = jnp.float32(0.0)
        for index in range(blocks):
            trace = trace + jnp.sum(jnp.where(diagonal, gram[band(index), band(index)], 0.0))
        shrink = jnp.where(
            step == 0, 1.0 / (jnp.sqrt(jnp.full((1, 1), trace)) + 1e-07), shrink
        )
        square = shrink * shrink

        @pl.when(opening)
        def _():
            scale = jnp.where(step == 0, square, jnp.ones_like(square))
            for index in range(blocks):
                scaled = gram[band(index), tail(index)] * scale
                gram[band(index), tail(index)] = scaled
                low[band(index), tail(index)] = scaled.astype(jnp.bfloat16)
            mirror(low)

        def keep_poly(index, squared):
            poly[band(index), tail(index)] = (
                slope * gram[band(index), tail(index)] + curve * squared
            ).astype(jnp.bfloat16)

        half_product(low, low, keep_poly)
        mirror(poly)
        newest = product.at[step % 2]
        older = product.at[(step + 1) % 2]

        @pl.when(opening)
        def _():
            newest[...] = poly[...]

        @pl.when(jnp.logical_not(opening))
        def _():
            def keep_product(index, multiplied):
                newest[band(index), tail(index)] = (
                    lead * older[band(index), tail(index)].astype(jnp.float32)
                    + lead_power * poly[band(index), tail(index)].astype(jnp.float32)
                    + multiplied
                ).astype(jnp.bfloat16)

            half_product(poly, older, keep_product)
            mirror(newest)

        lead_power = jnp.where(opening, jnp.float32(lead), lead_power * lead)

        @pl.when(step != GROUP - 1)
        def _():
            def keep_mixed(index, multiplied):
                grown = lead * gram[band(index), tail(index)] + multiplied
                mixed[band(index), tail(index)] = grown
                mixed_low[band(index), tail(index)] = grown.astype(jnp.bfloat16)

            half_product(poly, low, keep_mixed)

            @pl.when(step == GROUP)
            def _():
                for index in range(blocks):
                    older[band(index), tail(index)] = (
                        gram[band(index), tail(index)]
                        - low[band(index), tail(index)].astype(jnp.float32)
                    ).astype(jnp.bfloat16)
                mirror(older)

                def add_rest(index, multiplied):
                    grown = mixed[band(index), tail(index)] + multiplied
                    mixed[band(index), tail(index)] = grown
                    mixed_low[band(index), tail(index)] = grown.astype(jnp.bfloat16)

                half_product(poly, older, add_rest)

            mirror(mixed_low)

            def keep_gram(index, multiplied):
                fresh = lead * mixed[band(index), tail(index)] + multiplied
                gram[band(index), tail(index)] = fresh
                low[band(index), tail(index)] = fresh.astype(jnp.bfloat16)

            half_product(poly, mixed_low, keep_gram)
            mirror(low)

        @pl.when(step == GROUP - 1)
        def _():
            def advance(block, carry):
                here = pl.ds(pl.multiple_of(block * SLAB, SLAB), SLAB)
                moved = jnp.dot(newest[...], iterate[:, here], preferred_element_type=jnp.float32)
                iterate[:, here] = (
                    shrink * (lead_power * iterate[:, here].astype(jnp.float32) + moved)
                ).astype(jnp.bfloat16)
                return carry

            lax.fori_loop(0, iterate.shape[1] // SLAB, advance, 0)

        return lead_power, shrink

    lead_power, shrink = lax.fori_loop(
        0, SCHULZ - 1, sweep, (jnp.float32(1.0), jnp.ones((1, 1), jnp.float32))
    )
    last = product.at[(SCHULZ - 2) % 2]
    rest = product.at[(SCHULZ - 1) % 2]
    for index in range(blocks):
        rest[band(index), tail(index)] = (
            gram[band(index), tail(index)] - low[band(index), tail(index)].astype(jnp.float32)
        ).astype(jnp.bfloat16)
    mirror(rest)
    mine = pl.ds(pl.multiple_of(place[0] * rows, rows), rows)
    squared = jnp.dot(low[mine, :], low[...], preferred_element_type=jnp.float32)
    own_gram = low[mine, :].astype(jnp.float32) + rest[mine, :].astype(jnp.float32)
    own_poly = (slope * own_gram + curve * squared).astype(jnp.bfloat16)
    own_product = (
        lead * last[mine, :].astype(jnp.float32)
        + lead_power * own_poly.astype(jnp.float32)
        + jnp.dot(own_poly, last[...], preferred_element_type=jnp.float32)
    )
    own_high = own_product.astype(jnp.bfloat16)
    own_low = (own_product - own_high.astype(jnp.float32)).astype(jnp.bfloat16)
    for block in range(column_blocks):
        here = slice(block * columns, (block + 1) * columns)
        moved = jnp.dot(own_high, iterate[:, here], preferred_element_type=jnp.float32)
        moved = moved + jnp.dot(own_low, iterate[:, here], preferred_element_type=jnp.float32)
        result[block] = (
            (lead_power * lead) * iterate[mine, here].astype(jnp.float32) + moved
        ).astype(jnp.bfloat16)


def own_schulz(pieces, place):
    holders, column_blocks, rows, columns = pieces.shape
    width = holders * rows
    flops = 2 * width * width * (10 * width + 3 * column_blocks * columns)
    return pl.pallas_call(
        schulz_kernel,
        name="schulz",
        out_shape=jax.ShapeDtypeStruct((column_blocks, rows, columns), jnp.bfloat16),
        in_specs=[
            pl.BlockSpec(memory_space=pltpu.SMEM),
            pl.BlockSpec(memory_space=pl.ANY),
        ],
        out_specs=pl.BlockSpec(memory_space=pltpu.VMEM),
        scratch_shapes=[
            pltpu.VMEM((width, column_blocks * columns), jnp.bfloat16),
            pltpu.VMEM((width, width), jnp.float32),
            pltpu.VMEM((width, width), jnp.float32),
            pltpu.VMEM((width, width), jnp.bfloat16),
            pltpu.VMEM((width, width), jnp.bfloat16),
            pltpu.VMEM((width, width), jnp.bfloat16),
            pltpu.VMEM((2, width, width), jnp.bfloat16),
            pltpu.SemaphoreType.DMA((holders * column_blocks,)),
        ],
        compiler_params=pltpu.CompilerParams(vmem_limit_bytes=62 * 1024 * 1024),
        cost_estimate=pl.CostEstimate(
            flops=flops, bytes_accessed=4 * width * columns * column_blocks, transcendentals=0
        ),
    )(place, pieces)


def plain_update(weight, moment, gradient):
    fresh = moment_decay * moment + gradient
    return (weight - plain_rate * fresh, fresh)


def local(
    tokens,
    cotangent,
    lengths,
    gate_weight,
    inner_weight,
    output_weight,
    delta_weight,
    state_weight,
    inner_filter,
    state_filter,
    head_scalars,
    norm_gain,
    input_gain,
    gate_moment,
    inner_moment,
    output_moment,
    delta_moment,
    state_moment,
    inner_filter_moment,
    state_filter_moment,
    head_scalars_moment,
    norm_gain_moment,
    input_gain_moment,
):
    row_count = tokens.shape[0]
    segment, position = packing_layout(lengths[0], row_count)
    full_gate, full_inner, full_output, full_delta, full_state = (
        lax.all_gather(gate_weight.astype(jnp.bfloat16), "dp", axis=0, tiled=True),
        lax.all_gather(inner_weight.astype(jnp.bfloat16), "dp", axis=0, tiled=True),
        lax.all_gather(output_weight.astype(jnp.bfloat16), "dp", axis=0, tiled=True),
        lax.all_gather(delta_weight.astype(jnp.bfloat16), "dp", axis=0, tiled=True),
        lax.all_gather(state_weight.astype(jnp.bfloat16), "dp", axis=0, tiled=True),
    )
    columns = full_gate.shape[1]
    head_count = full_delta.shape[1]
    mixing_cols = 2 * columns + head_count
    in_matrix = jnp.concatenate([full_gate, full_inner, full_delta, full_state], axis=1)
    tokens_wide = tokens.astype(jnp.float32)
    root_scale = lax.rsqrt(
        jnp.mean(tokens_wide * tokens_wide, axis=1, keepdims=True) + norm_epsilon
    )
    normed = (tokens_wide * root_scale * input_gain).astype(jnp.bfloat16)
    projected = jnp.dot(normed, in_matrix, preferred_element_type=jnp.float32)
    gate_part = projected[:, :columns]
    inner_part = projected[:, columns : 2 * columns]
    delta_raw = projected[:, 2 * columns : mixing_cols]
    state_raw = projected[:, mixing_cols:]

    def state_rows(raw_values, taps):
        filtered = causal_filter(raw_values, taps, position)
        return (filtered[:, :NSTATE], filtered[:, NSTATE:])

    def mixer(gate_in, inner_in, delta_in, entry_in, readout_in, taps, scalars):
        return state_mixer(
            gate_in, inner_in, delta_in, entry_in, readout_in, taps, scalars, segment, position
        )

    (entry_rows, readout_rows), state_back = jax.vjp(state_rows, state_raw, state_filter)
    gated, mixer_back = jax.vjp(
        mixer,
        gate_part,
        inner_part,
        delta_raw,
        entry_rows,
        readout_rows,
        inner_filter,
        head_scalars,
    )
    squares = lax.psum(jnp.sum(gated * gated, axis=1), "tensor")
    norm_scale = lax.rsqrt(squares / INNER + norm_epsilon)[:, None]
    normalized = (gated * norm_scale * norm_gain).astype(jnp.bfloat16)
    partial_out = jnp.einsum(
        "ti,di->td", normalized, full_output, preferred_element_type=jnp.float32
    )
    block_output = (tokens_wide + lax.psum(partial_out, "tensor")).astype(jnp.bfloat16)
    grad_normalized = jnp.dot(cotangent, full_output, preferred_element_type=jnp.float32)
    output_local = jnp.einsum(
        "td,ti->di", cotangent, normalized, preferred_element_type=jnp.float32
    )
    norm_gain_local = jnp.sum(grad_normalized * gated * norm_scale, axis=0)
    weighted = grad_normalized * norm_gain
    inner_dot = lax.psum(jnp.sum(weighted * gated, axis=1), "tensor")
    grad_gated = norm_scale * weighted - gated * norm_scale**3 * (inner_dot / INNER)[:, None]
    grad_gate, grad_inner, grad_delta, grad_entry, grad_readout, filter_local, scalar_local = (
        mixer_back(grad_gated)
    )
    entry_total, readout_total = lax.psum((grad_entry, grad_readout), "tensor")
    grad_state, state_filter_local = state_back((entry_total, readout_total))
    grad_mixing = jnp.concatenate([grad_gate, grad_inner, grad_delta], axis=1).astype(jnp.bfloat16)
    grad_state_low = grad_state.astype(jnp.bfloat16)
    input_partial = jnp.einsum(
        "tk,dk->td", grad_mixing, in_matrix[:, :mixing_cols], preferred_element_type=jnp.float32
    )
    mixing_weight_grad = jnp.einsum(
        "td,tk->dk", normed, grad_mixing, preferred_element_type=jnp.float32
    )
    state_local = jnp.einsum(
        "td,tk->dk", normed, grad_state_low, preferred_element_type=jnp.float32
    )
    state_input = jnp.einsum(
        "tk,dk->td", grad_state_low, full_state, preferred_element_type=jnp.float32
    )
    grad_normed = lax.psum(input_partial, "tensor") + state_input
    input_gain_local = jnp.sum(grad_normed * tokens_wide * root_scale, axis=0)
    weighted_in = grad_normed * input_gain
    row_mean = jnp.mean(weighted_in * tokens_wide, axis=1, keepdims=True)
    input_gradient = (
        cotangent.astype(jnp.float32)
        + root_scale * weighted_in
        - tokens_wide * root_scale**3 * row_mean
    )
    def scattered(partial):
        low = partial.astype(jnp.bfloat16)
        return lax.psum_scatter(low, "dp", scatter_dimension=0, tiled=True).astype(jnp.float32)

    output_sum = scattered(output_local)
    gate_sum = scattered(mixing_weight_grad[:, :columns])
    inner_sum = scattered(mixing_weight_grad[:, columns : 2 * columns])
    delta_sum = lax.psum_scatter(
        mixing_weight_grad[:, 2 * columns :], "dp", scatter_dimension=0, tiled=True
    )
    state_sum = lax.psum_scatter(state_local, "dp", scatter_dimension=0, tiled=True)
    filter_sum, state_filter_sum, scalar_sum, norm_gain_sum, input_gain_sum = lax.psum(
        (filter_local, state_filter_local, scalar_local, norm_gain_local, input_gain_local), "dp"
    )
    fresh_stack = moment_decay * jnp.stack([gate_moment, inner_moment, output_moment]) + jnp.stack(
        [gate_sum, inner_sum, output_sum]
    )
    spare = jnp.zeros((lax.axis_size("tensor") - 3,) + fresh_stack.shape[1:], jnp.bfloat16)
    rounded_stack = jnp.concatenate([fresh_stack.astype(jnp.bfloat16), spare], axis=0)
    own_rows = lax.all_to_all(rounded_stack, "tensor", split_axis=0, concat_axis=0, tiled=True)
    whole = lax.all_gather(own_rows, "dp", axis=0)
    produced = own_schulz(whole, lax.axis_index("dp").reshape(1).astype(jnp.int32))
    ortho = lax.all_to_all(produced, "tensor", split_axis=0, concat_axis=0, tiled=True)[:3]
    factor = 0.2 * math.sqrt(max(D, INNER))
    muon_new = jnp.stack(
        [gate_weight, inner_weight, output_weight]
    ) - muon_rate * factor * ortho.astype(jnp.float32)
    delta_updated, delta_moment_new = plain_update(delta_weight, delta_moment, delta_sum)
    state_updated, state_moment_new = plain_update(state_weight, state_moment, state_sum)
    filter_updated, filter_moment_new = plain_update(inner_filter, inner_filter_moment, filter_sum)
    state_filter_updated, state_filter_moment_new = plain_update(
        state_filter, state_filter_moment, state_filter_sum
    )
    scalar_updated, scalar_moment_new = plain_update(head_scalars, head_scalars_moment, scalar_sum)
    norm_gain_updated, norm_gain_moment_new = plain_update(
        norm_gain, norm_gain_moment, norm_gain_sum
    )
    input_gain_updated, input_gain_moment_new = plain_update(
        input_gain, input_gain_moment, input_gain_sum
    )
    return (
        block_output,
        input_gradient,
        gate_sum,
        inner_sum,
        output_sum,
        delta_sum,
        state_sum,
        filter_sum,
        state_filter_sum,
        scalar_sum,
        norm_gain_sum,
        input_gain_sum,
        muon_new[0],
        muon_new[1],
        muon_new[2],
        delta_updated,
        state_updated,
        filter_updated,
        state_filter_updated,
        scalar_updated,
        norm_gain_updated,
        input_gain_updated,
        fresh_stack[0],
        fresh_stack[1],
        fresh_stack[2],
        delta_moment_new,
        state_moment_new,
        filter_moment_new,
        state_filter_moment_new,
        scalar_moment_new,
        norm_gain_moment_new,
        input_gain_moment_new,
    )


def solution(mesh):
    placed = (
        P("dp", None),
        P("dp", None),
        P("dp", None),
        P("dp", "tensor"),
        P("dp", "tensor"),
        P("dp", "tensor"),
        P("dp", "tensor"),
        P("dp", None),
        P(None, "tensor"),
        P(),
        P(None, "tensor"),
        P("tensor"),
        P(),
        P("dp", "tensor"),
        P("dp", "tensor"),
        P("dp", "tensor"),
        P("dp", "tensor"),
        P("dp", None),
        P(None, "tensor"),
        P(),
        P(None, "tensor"),
        P("tensor"),
        P(),
    )
    return jax.shard_map(
        local,
        mesh=mesh,
        in_specs=placed,
        out_specs=(
            P("dp", None),
            P("dp", None),
            P("dp", "tensor"),
            P("dp", "tensor"),
            P("dp", "tensor"),
            P("dp", "tensor"),
            P("dp", None),
            P(None, "tensor"),
            P(),
            P(None, "tensor"),
            P("tensor"),
            P(),
            P("dp", "tensor"),
            P("dp", "tensor"),
            P("dp", "tensor"),
            P("dp", "tensor"),
            P("dp", None),
            P(None, "tensor"),
            P(),
            P(None, "tensor"),
            P("tensor"),
            P(),
            P("dp", "tensor"),
            P("dp", "tensor"),
            P("dp", "tensor"),
            P("dp", "tensor"),
            P("dp", None),
            P(None, "tensor"),
            P(),
            P(None, "tensor"),
            P("tensor"),
            P(),
        ),
        check_vma=False,
    )
```

```python
import math

import jax
import jax.numpy as jnp
from jax import lax
from jax.experimental import pallas as pl
from jax.experimental.pallas import tpu as pltpu
from jax.sharding import PartitionSpec as P

D = 1536
INNER = 3072
NSTATE = 128
CONV = 4
SPAN = 256
SCHULZ = 5
GROUP = 3
TILE = 256
SLAB = 512


norm_epsilon = 1e-05
moment_decay = 0.95
muon_rate = 0.02
plain_rate = 0.002
schulz_terms = (3.4445, -4.775, 2.0315)
exact_mode = lax.Precision.HIGHEST


def packing_layout(length_row, row_count):
    ends = jnp.cumsum(length_row)
    places = jnp.arange(row_count, dtype=jnp.int32)
    after = (places[:, None] >= ends[None, :]).astype(jnp.int32)
    segment = jnp.sum(after, axis=1)
    starts = jnp.sum(after * length_row[None, :], axis=1)
    return (segment, places - starts)


def shifted_rows(values, offset):
    padding = jnp.zeros((offset, values.shape[1]), values.dtype)
    return jnp.concatenate([padding, values[: values.shape[0] - offset]], axis=0)


def causal_filter(values, taps, position):
    summed = taps[CONV] + taps[CONV - 1] * values
    for offset in range(1, CONV):
        inside = (position >= offset).astype(jnp.float32)[:, None]
        summed = summed + taps[CONV - 1 - offset] * shifted_rows(values, offset) * inside
    return jax.nn.silu(summed)


def state_mixer(
    gate_part,
    inner_part,
    delta_raw,
    entry_rows,
    readout_rows,
    inner_filter,
    head_scalars,
    segment,
    position,
):
    row_count, head_count = delta_raw.shape
    head_width = inner_part.shape[1] // head_count
    block_count = row_count // SPAN
    filtered = causal_filter(inner_part, inner_filter, position)
    delta_step = jax.nn.softplus(delta_raw + head_scalars[0])
    step_log = delta_step * -jnp.exp(head_scalars[1])
    heads_in = filtered.reshape(row_count, head_count, head_width)
    driven = (heads_in * delta_step[:, :, None]).reshape(block_count, SPAN, head_count, head_width)
    lower_mask = (jnp.arange(SPAN)[:, None] >= jnp.arange(SPAN)[None, :]).astype(jnp.float32)
    running = jnp.einsum(
        "ij,cjh->cih",
        lower_mask,
        step_log.reshape(block_count, SPAN, head_count),
        precision=exact_mode,
    )
    block_seg = segment.reshape(block_count, SPAN)
    same_seq = (block_seg[:, :, None] == block_seg[:, None, :]).astype(jnp.float32) * lower_mask
    spread = running[:, :, None, :] - running[:, None, :, :]
    entry_blocks = entry_rows.reshape(block_count, SPAN, -1)
    readout_blocks = readout_rows.reshape(block_count, SPAN, -1)
    correlation = jnp.einsum("cin,cjn->cij", readout_blocks, entry_blocks, precision=exact_mode)
    mixing = jnp.exp(jnp.minimum(spread, 0.0)) * (correlation * same_seq)[:, :, :, None]
    within = jnp.einsum("cijh,cjhp->cihp", mixing, driven, precision=exact_mode)
    final_log = running[:, -1, :]
    last_seg = block_seg[:, -1]
    tail_weight = (
        jnp.exp(final_log[:, None, :] - running)
        * (block_seg == last_seg[:, None]).astype(jnp.float32)[:, :, None]
    )
    fresh_states = jnp.einsum(
        "cjh,cjhp,cjn->chpn", tail_weight, driven, entry_blocks, precision=exact_mode
    )
    prior_seg = jnp.concatenate([jnp.full((1,), -1, dtype=jnp.int32), last_seg[:-1]])
    carry_keep = (last_seg == prior_seg).astype(jnp.float32)

    def advance(carried_state, pieces):
        keep_flag, total_log, update = pieces
        return (
            keep_flag * jnp.exp(total_log)[:, None, None] * carried_state + update,
            carried_state,
        )

    start_state = jnp.zeros(fresh_states.shape[1:], jnp.float32)
    final_state, entering = lax.scan(advance, start_state, (carry_keep, final_log, fresh_states))
    reach_weight = (
        jnp.exp(running) * (block_seg == prior_seg[:, None]).astype(jnp.float32)[:, :, None]
    )
    carried = jnp.einsum(
        "cih,cin,chpn->cihp", reach_weight, readout_blocks, entering, precision=exact_mode
    )
    outputs = (within + carried).reshape(row_count, head_count, head_width) + head_scalars[2][
        None, :, None
    ] * heads_in
    return outputs.reshape(row_count, head_count * head_width) * jax.nn.silu(gate_part)


def schulz_kernel(
    place, pieces, result, iterate, gram, mixed, low, poly, mixed_low, product, arrived
):
    holders, column_blocks, rows, columns = pieces.shape
    width = iterate.shape[0]
    blocks = width // TILE
    lead, slope, curve = schulz_terms

    def piece_copy(index):
        holder = index // column_blocks
        block = index % column_blocks
        return pltpu.make_async_copy(
            pieces.at[holder, block],
            iterate.at[
                pl.ds(pl.multiple_of(holder * rows, rows), rows),
                pl.ds(pl.multiple_of(block * columns, columns), columns),
            ],
            arrived.at[index],
        )

    def begin(index, carry):
        piece_copy(index).start()
        return carry

    def finish(index, carry):
        piece_copy(index).wait()
        return carry

    lax.fori_loop(0, holders * column_blocks, begin, 0)
    lax.fori_loop(0, holders * column_blocks, finish, 0)
    unit_rows = lax.broadcasted_iota(jnp.int32, (TILE, TILE), 0)
    unit_columns = lax.broadcasted_iota(jnp.int32, (TILE, TILE), 1)
    diagonal = unit_rows == unit_columns
    unit = jnp.where(diagonal, 1.0, 0.0).astype(jnp.bfloat16)

    def band(index):
        return slice(index * TILE, (index + 1) * TILE)

    def tail(index):
        return slice(index * TILE, width)

    def mirror(target):
        for upper in range(blocks):
            for right in range(upper + 1, blocks):
                flipped = lax.dot_general(
                    unit,
                    target[band(upper), band(right)],
                    (((1,), (1,)), ((), ())),
                    preferred_element_type=jnp.float32,
                )
                target[band(right), band(upper)] = flipped.astype(jnp.bfloat16)

    def half_product(left, right, finish_band):
        for index in range(blocks):
            finish_band(
                index,
                jnp.dot(
                    left[band(index), :],
                    right[:, tail(index)],
                    preferred_element_type=jnp.float32,
                ),
            )

    def sweep(step, carry):
        lead_power, shrink = carry
        opening = (step == 0) | (step == GROUP)

        @pl.when(opening)
        def _():
            for index in range(blocks):
                gram[band(index), tail(index)] = lax.dot_general(
                    iterate[band(index), :],
                    iterate[tail(index), :],
                    (((1,), (1,)), ((), ())),
                    preferred_element_type=jnp.float32,
                )

        trace = jnp.float32(0.0)
        for index in range(blocks):
            trace = trace + jnp.sum(jnp.where(diagonal, gram[band(index), band(index)], 0.0))
        shrink = jnp.where(
            step == 0, 1.0 / (jnp.sqrt(jnp.full((1, 1), trace)) + 1e-07), shrink
        )
        square = shrink * shrink

        @pl.when(opening)
        def _():
            scale = jnp.where(step == 0, square, jnp.ones_like(square))
            for index in range(blocks):
                scaled = gram[band(index), tail(index)] * scale
                gram[band(index), tail(index)] = scaled
                low[band(index), tail(index)] = scaled.astype(jnp.bfloat16)
            mirror(low)

        def keep_poly(index, squared):
            poly[band(index), tail(index)] = (
                slope * gram[band(index), tail(index)] + curve * squared
            ).astype(jnp.bfloat16)

        half_product(low, low, keep_poly)
        mirror(poly)
        newest = product.at[step % 2]
        older = product.at[(step + 1) % 2]

        @pl.when(opening)
        def _():
            newest[...] = poly[...]

        @pl.when(jnp.logical_not(opening))
        def _():
            def keep_product(index, multiplied):
                newest[band(index), tail(index)] = (
                    lead * older[band(index), tail(index)].astype(jnp.float32)
                    + lead_power * poly[band(index), tail(index)].astype(jnp.float32)
                    + multiplied
                ).astype(jnp.bfloat16)

            half_product(poly, older, keep_product)
            mirror(newest)

        lead_power = jnp.where(opening, jnp.float32(lead), lead_power * lead)

        @pl.when(step != GROUP - 1)
        def _():
            def keep_mixed(index, multiplied):
                grown = lead * gram[band(index), tail(index)] + multiplied
                mixed[band(index), tail(index)] = grown
                mixed_low[band(index), tail(index)] = grown.astype(jnp.bfloat16)

            half_product(poly, low, keep_mixed)

            @pl.when(step == GROUP)
            def _():
                for index in range(blocks):
                    older[band(index), tail(index)] = (
                        gram[band(index), tail(index)]
                        - low[band(index), tail(index)].astype(jnp.float32)
                    ).astype(jnp.bfloat16)
                mirror(older)

                def add_rest(index, multiplied):
                    grown = mixed[band(index), tail(index)] + multiplied
                    mixed[band(index), tail(index)] = grown
                    mixed_low[band(index), tail(index)] = grown.astype(jnp.bfloat16)

                half_product(poly, older, add_rest)

            mirror(mixed_low)

            def keep_gram(index, multiplied):
                fresh = lead * mixed[band(index), tail(index)] + multiplied
                gram[band(index), tail(index)] = fresh
                low[band(index), tail(index)] = fresh.astype(jnp.bfloat16)

            half_product(poly, mixed_low, keep_gram)
            mirror(low)

        @pl.when(step == GROUP - 1)
        def _():
            def advance(block, carry):
                here = pl.ds(pl.multiple_of(block * SLAB, SLAB), SLAB)
                moved = jnp.dot(newest[...], iterate[:, here], preferred_element_type=jnp.float32)
                iterate[:, here] = (
                    shrink * (lead_power * iterate[:, here].astype(jnp.float32) + moved)
                ).astype(jnp.bfloat16)
                return carry

            lax.fori_loop(0, iterate.shape[1] // SLAB, advance, 0)

        return lead_power, shrink

    lead_power, shrink = lax.fori_loop(
        0, SCHULZ - 1, sweep, (jnp.float32(1.0), jnp.ones((1, 1), jnp.float32))
    )
    last = product.at[(SCHULZ - 2) % 2]
    rest = product.at[(SCHULZ - 1) % 2]
    for index in range(blocks):
        rest[band(index), tail(index)] = (
            gram[band(index), tail(index)] - low[band(index), tail(index)].astype(jnp.float32)
        ).astype(jnp.bfloat16)
    mirror(rest)
    mine = pl.ds(pl.multiple_of(place[0] * rows, rows), rows)
    squared = jnp.dot(low[mine, :], low[...], preferred_element_type=jnp.float32)
    own_gram = low[mine, :].astype(jnp.float32) + rest[mine, :].astype(jnp.float32)
    own_poly = (slope * own_gram + curve * squared).astype(jnp.bfloat16)
    own_product = (
        lead * last[mine, :].astype(jnp.float32)
        + lead_power * own_poly.astype(jnp.float32)
        + jnp.dot(own_poly, last[...], preferred_element_type=jnp.float32)
    )
    own_high = own_product.astype(jnp.bfloat16)
    own_low = (own_product - own_high.astype(jnp.float32)).astype(jnp.bfloat16)
    halves = jnp.concatenate([own_high, own_low], axis=0)
    for block in range(column_blocks):
        here = slice(block * columns, (block + 1) * columns)
        moved = jnp.dot(halves, iterate[:, here], preferred_element_type=jnp.float32)
        result[block] = (
            (lead_power * lead) * iterate[mine, here].astype(jnp.float32)
            + (moved[:rows] + moved[rows:])
        ).astype(jnp.bfloat16)


def own_schulz(pieces, place):
    holders, column_blocks, rows, columns = pieces.shape
    width = holders * rows
    flops = 2 * width * width * (10 * width + 3 * column_blocks * columns)
    return pl.pallas_call(
        schulz_kernel,
        name="schulz",
        out_shape=jax.ShapeDtypeStruct((column_blocks, rows, columns), jnp.bfloat16),
        in_specs=[
            pl.BlockSpec(memory_space=pltpu.SMEM),
            pl.BlockSpec(memory_space=pl.ANY),
        ],
        out_specs=pl.BlockSpec(memory_space=pltpu.VMEM),
        scratch_shapes=[
            pltpu.VMEM((width, column_blocks * columns), jnp.bfloat16),
            pltpu.VMEM((width, width), jnp.float32),
            pltpu.VMEM((width, width), jnp.float32),
            pltpu.VMEM((width, width), jnp.bfloat16),
            pltpu.VMEM((width, width), jnp.bfloat16),
            pltpu.VMEM((width, width), jnp.bfloat16),
            pltpu.VMEM((2, width, width), jnp.bfloat16),
            pltpu.SemaphoreType.DMA((holders * column_blocks,)),
        ],
        compiler_params=pltpu.CompilerParams(vmem_limit_bytes=62 * 1024 * 1024),
        cost_estimate=pl.CostEstimate(
            flops=flops, bytes_accessed=4 * width * columns * column_blocks, transcendentals=0
        ),
    )(place, pieces)


def plain_update(weight, moment, gradient):
    fresh = moment_decay * moment + gradient
    return (weight - plain_rate * fresh, fresh)


def local(
    tokens,
    cotangent,
    lengths,
    gate_weight,
    inner_weight,
    output_weight,
    delta_weight,
    state_weight,
    inner_filter,
    state_filter,
    head_scalars,
    norm_gain,
    input_gain,
    gate_moment,
    inner_moment,
    output_moment,
    delta_moment,
    state_moment,
    inner_filter_moment,
    state_filter_moment,
    head_scalars_moment,
    norm_gain_moment,
    input_gain_moment,
):
    row_count = tokens.shape[0]
    segment, position = packing_layout(lengths[0], row_count)
    full_gate, full_inner, full_output, full_delta, full_state = (
        lax.all_gather(gate_weight.astype(jnp.bfloat16), "dp", axis=0, tiled=True),
        lax.all_gather(inner_weight.astype(jnp.bfloat16), "dp", axis=0, tiled=True),
        lax.all_gather(output_weight.astype(jnp.bfloat16), "dp", axis=0, tiled=True),
        lax.all_gather(delta_weight.astype(jnp.bfloat16), "dp", axis=0, tiled=True),
        lax.all_gather(state_weight.astype(jnp.bfloat16), "dp", axis=0, tiled=True),
    )
    columns = full_gate.shape[1]
    head_count = full_delta.shape[1]
    mixing_cols = 2 * columns + head_count
    in_matrix = jnp.concatenate([full_gate, full_inner, full_delta, full_state], axis=1)
    tokens_wide = tokens.astype(jnp.float32)
    root_scale = lax.rsqrt(
        jnp.mean(tokens_wide * tokens_wide, axis=1, keepdims=True) + norm_epsilon
    )
    normed = (tokens_wide * root_scale * input_gain).astype(jnp.bfloat16)
    projected = jnp.dot(normed, in_matrix, preferred_element_type=jnp.float32)
    gate_part = projected[:, :columns]
    inner_part = projected[:, columns : 2 * columns]
    delta_raw = projected[:, 2 * columns : mixing_cols]
    state_raw = projected[:, mixing_cols:]

    def state_rows(raw_values, taps):
        filtered = causal_filter(raw_values, taps, position)
        return (filtered[:, :NSTATE], filtered[:, NSTATE:])

    def mixer(gate_in, inner_in, delta_in, entry_in, readout_in, taps, scalars):
        return state_mixer(
            gate_in, inner_in, delta_in, entry_in, readout_in, taps, scalars, segment, position
        )

    (entry_rows, readout_rows), state_back = jax.vjp(state_rows, state_raw, state_filter)
    gated, mixer_back = jax.vjp(
        mixer,
        gate_part,
        inner_part,
        delta_raw,
        entry_rows,
        readout_rows,
        inner_filter,
        head_scalars,
    )
    grad_normalized = jnp.dot(cotangent, full_output, preferred_element_type=jnp.float32)
    weighted = grad_normalized * norm_gain
    squares, inner_dot = lax.psum(
        jnp.stack([jnp.sum(gated * gated, axis=1), jnp.sum(weighted * gated, axis=1)]), "tensor"
    )
    norm_scale = lax.rsqrt(squares / INNER + norm_epsilon)[:, None]
    normalized = (gated * norm_scale * norm_gain).astype(jnp.bfloat16)
    partial_out = jnp.einsum(
        "ti,di->td", normalized, full_output, preferred_element_type=jnp.float32
    )
    output_local = jnp.einsum(
        "td,ti->di", cotangent, normalized, preferred_element_type=jnp.float32
    )
    norm_gain_local = jnp.sum(grad_normalized * gated * norm_scale, axis=0)
    grad_gated = norm_scale * weighted - gated * norm_scale**3 * (inner_dot / INNER)[:, None]
    grad_gate, grad_inner, grad_delta, grad_entry, grad_readout, filter_local, scalar_local = (
        mixer_back(grad_gated)
    )
    entry_total, readout_total = lax.psum((grad_entry, grad_readout), "tensor")
    grad_state, state_filter_local = state_back((entry_total, readout_total))
    grad_mixing = jnp.concatenate([grad_gate, grad_inner, grad_delta], axis=1).astype(jnp.bfloat16)
    grad_state_low = grad_state.astype(jnp.bfloat16)
    input_partial = jnp.einsum(
        "tk,dk->td", grad_mixing, in_matrix[:, :mixing_cols], preferred_element_type=jnp.float32
    )
    mixing_weight_grad = jnp.einsum(
        "td,tk->dk", normed, grad_mixing, preferred_element_type=jnp.float32
    )
    state_local = jnp.einsum(
        "td,tk->dk", normed, grad_state_low, preferred_element_type=jnp.float32
    )
    state_input = jnp.einsum(
        "tk,dk->td", grad_state_low, full_state, preferred_element_type=jnp.float32
    )
    input_gain_local = jnp.sum(
        (input_partial + state_input / lax.axis_size("tensor")) * tokens_wide * root_scale, axis=0
    )

    def scattered(partial):
        low = partial.astype(jnp.bfloat16)
        return lax.psum_scatter(low, "dp", scatter_dimension=0, tiled=True).astype(jnp.float32)

    output_sum = scattered(output_local)
    gate_sum = scattered(mixing_weight_grad[:, :columns])
    inner_sum = scattered(mixing_weight_grad[:, columns : 2 * columns])
    filter_sum, state_filter_sum, scalar_sum, norm_gain_sum = lax.psum(
        (filter_local, state_filter_local, scalar_local, norm_gain_local), "dp"
    )
    input_gain_sum = lax.psum(input_gain_local, ("dp", "tensor"))
    fresh_stack = moment_decay * jnp.stack([gate_moment, inner_moment, output_moment]) + jnp.stack(
        [gate_sum, inner_sum, output_sum]
    )
    spare = jnp.zeros((lax.axis_size("tensor") - 3,) + fresh_stack.shape[1:], jnp.bfloat16)
    rounded_stack = jnp.concatenate([fresh_stack.astype(jnp.bfloat16), spare], axis=0)
    (
        rounded_stack,
        filter_sum,
        state_filter_sum,
        scalar_sum,
        norm_gain_sum,
        input_gain_sum,
    ) = lax.optimization_barrier(
        (
            rounded_stack,
            filter_sum,
            state_filter_sum,
            scalar_sum,
            norm_gain_sum,
            input_gain_sum,
        )
    )
    own_rows = lax.all_to_all(rounded_stack, "tensor", split_axis=0, concat_axis=0, tiled=True)
    whole = lax.all_gather(own_rows, "dp", axis=0)
    side = jnp.concatenate([state_local, mixing_weight_grad[:, 2 * columns :]], axis=1)
    whole, out_low, input_low, side = lax.optimization_barrier(
        (whole, partial_out.astype(jnp.bfloat16), input_partial.astype(jnp.bfloat16), side)
    )
    out_total, input_total = lax.psum((out_low, input_low), "tensor")
    side_sum = lax.psum_scatter(side, "dp", scatter_dimension=0, tiled=True)
    produced = own_schulz(whole, lax.axis_index("dp").reshape(1).astype(jnp.int32))
    out_total, input_total, side_sum, _ = lax.optimization_barrier(
        (out_total, input_total, side_sum, produced[0, :16, :128])
    )
    ortho = lax.all_to_all(produced, "tensor", split_axis=0, concat_axis=0, tiled=True)[:3]
    state_sum = side_sum[:, : 2 * NSTATE]
    delta_sum = side_sum[:, 2 * NSTATE :]
    block_output = (tokens_wide + out_total.astype(jnp.float32)).astype(jnp.bfloat16)
    grad_normed = input_total.astype(jnp.float32) + state_input
    weighted_in = grad_normed * input_gain
    row_mean = jnp.mean(weighted_in * tokens_wide, axis=1, keepdims=True)
    input_gradient = (
        cotangent.astype(jnp.float32)
        + root_scale * weighted_in
        - tokens_wide * root_scale**3 * row_mean
    )
    factor = 0.2 * math.sqrt(max(D, INNER))
    muon_new = jnp.stack(
        [gate_weight, inner_weight, output_weight]
    ) - muon_rate * factor * ortho.astype(jnp.float32)
    delta_updated, delta_moment_new = plain_update(delta_weight, delta_moment, delta_sum)
    state_updated, state_moment_new = plain_update(state_weight, state_moment, state_sum)
    filter_updated, filter_moment_new = plain_update(inner_filter, inner_filter_moment, filter_sum)
    state_filter_updated, state_filter_moment_new = plain_update(
        state_filter, state_filter_moment, state_filter_sum
    )
    scalar_updated, scalar_moment_new = plain_update(head_scalars, head_scalars_moment, scalar_sum)
    norm_gain_updated, norm_gain_moment_new = plain_update(
        norm_gain, norm_gain_moment, norm_gain_sum
    )
    input_gain_updated, input_gain_moment_new = plain_update(
        input_gain, input_gain_moment, input_gain_sum
    )
    return (
        block_output,
        input_gradient,
        gate_sum,
        inner_sum,
        output_sum,
        delta_sum,
        state_sum,
        filter_sum,
        state_filter_sum,
        scalar_sum,
        norm_gain_sum,
        input_gain_sum,
        muon_new[0],
        muon_new[1],
        muon_new[2],
        delta_updated,
        state_updated,
        filter_updated,
        state_filter_updated,
        scalar_updated,
        norm_gain_updated,
        input_gain_updated,
        fresh_stack[0],
        fresh_stack[1],
        fresh_stack[2],
        delta_moment_new,
        state_moment_new,
        filter_moment_new,
        state_filter_moment_new,
        scalar_moment_new,
        norm_gain_moment_new,
        input_gain_moment_new,
    )


def solution(mesh):
    placed = (
        P("dp", None),
        P("dp", None),
        P("dp", None),
        P("dp", "tensor"),
        P("dp", "tensor"),
        P("dp", "tensor"),
        P("dp", "tensor"),
        P("dp", None),
        P(None, "tensor"),
        P(),
        P(None, "tensor"),
        P("tensor"),
        P(),
        P("dp", "tensor"),
        P("dp", "tensor"),
        P("dp", "tensor"),
        P("dp", "tensor"),
        P("dp", None),
        P(None, "tensor"),
        P(),
        P(None, "tensor"),
        P("tensor"),
        P(),
    )
    return jax.shard_map(
        local,
        mesh=mesh,
        in_specs=placed,
        out_specs=(
            P("dp", None),
            P("dp", None),
            P("dp", "tensor"),
            P("dp", "tensor"),
            P("dp", "tensor"),
            P("dp", "tensor"),
            P("dp", None),
            P(None, "tensor"),
            P(),
            P(None, "tensor"),
            P("tensor"),
            P(),
            P("dp", "tensor"),
            P("dp", "tensor"),
            P("dp", "tensor"),
            P("dp", "tensor"),
            P("dp", None),
            P(None, "tensor"),
            P(),
            P(None, "tensor"),
            P("tensor"),
            P(),
            P("dp", "tensor"),
            P("dp", "tensor"),
            P("dp", "tensor"),
            P("dp", "tensor"),
            P("dp", None),
            P(None, "tensor"),
            P(),
            P(None, "tensor"),
            P("tensor"),
            P(),
        ),
        check_vma=False,
    )
```

```python
import math

import jax
import jax.numpy as jnp
from jax import lax
from jax.experimental import pallas as pl
from jax.experimental.pallas import tpu as pltpu
from jax.sharding import PartitionSpec as P

D = 1536
INNER = 3072
NSTATE = 128
CONV = 4
SPAN = 256
SCHULZ = 5
GROUP = 3
TILE = 256
SLAB = 512


norm_epsilon = 1e-05
moment_decay = 0.95
muon_rate = 0.02
plain_rate = 0.002
schulz_terms = (3.4445, -4.775, 2.0315)
exact_mode = lax.Precision.HIGHEST


def packing_layout(length_row, row_count):
    ends = jnp.cumsum(length_row)
    places = jnp.arange(row_count, dtype=jnp.int32)
    after = (places[:, None] >= ends[None, :]).astype(jnp.int32)
    segment = jnp.sum(after, axis=1)
    starts = jnp.sum(after * length_row[None, :], axis=1)
    return (segment, places - starts)


def shifted_rows(values, offset):
    padding = jnp.zeros((offset, values.shape[1]), values.dtype)
    return jnp.concatenate([padding, values[: values.shape[0] - offset]], axis=0)


def causal_filter(values, taps, position):
    summed = taps[CONV] + taps[CONV - 1] * values
    for offset in range(1, CONV):
        inside = (position >= offset).astype(jnp.float32)[:, None]
        summed = summed + taps[CONV - 1 - offset] * shifted_rows(values, offset) * inside
    return jax.nn.silu(summed)


def state_mixer(
    inner_part,
    delta_raw,
    entry_rows,
    readout_rows,
    inner_filter,
    head_scalars,
    segment,
    position,
):
    row_count, head_count = delta_raw.shape
    head_width = inner_part.shape[1] // head_count
    block_count = row_count // SPAN
    filtered = causal_filter(inner_part, inner_filter, position)
    delta_step = jax.nn.softplus(delta_raw + head_scalars[0])
    step_log = delta_step * -jnp.exp(head_scalars[1])
    heads_in = filtered.reshape(row_count, head_count, head_width)
    driven = (heads_in * delta_step[:, :, None]).reshape(block_count, SPAN, head_count, head_width)
    lower_mask = (jnp.arange(SPAN)[:, None] >= jnp.arange(SPAN)[None, :]).astype(jnp.float32)
    running = jnp.einsum(
        "ij,cjh->cih",
        lower_mask,
        step_log.reshape(block_count, SPAN, head_count),
        precision=exact_mode,
    )
    block_seg = segment.reshape(block_count, SPAN)
    same_seq = (block_seg[:, :, None] == block_seg[:, None, :]).astype(jnp.float32) * lower_mask
    spread = running[:, :, None, :] - running[:, None, :, :]
    entry_blocks = entry_rows.reshape(block_count, SPAN, -1)
    readout_blocks = readout_rows.reshape(block_count, SPAN, -1)
    correlation = jnp.einsum("cin,cjn->cij", readout_blocks, entry_blocks, precision=exact_mode)
    mixing = jnp.exp(jnp.minimum(spread, 0.0)) * (correlation * same_seq)[:, :, :, None]
    within = jnp.einsum("cijh,cjhp->cihp", mixing, driven, precision=exact_mode)
    final_log = running[:, -1, :]
    last_seg = block_seg[:, -1]
    tail_weight = (
        jnp.exp(final_log[:, None, :] - running)
        * (block_seg == last_seg[:, None]).astype(jnp.float32)[:, :, None]
    )
    fresh_states = jnp.einsum(
        "cjh,cjhp,cjn->chpn", tail_weight, driven, entry_blocks, precision=exact_mode
    )
    prior_seg = jnp.concatenate([jnp.full((1,), -1, dtype=jnp.int32), last_seg[:-1]])
    carry_keep = (last_seg == prior_seg).astype(jnp.float32)

    def advance(carried_state, pieces):
        keep_flag, total_log, update = pieces
        return (
            keep_flag * jnp.exp(total_log)[:, None, None] * carried_state + update,
            carried_state,
        )

    start_state = jnp.zeros(fresh_states.shape[1:], jnp.float32)
    final_state, entering = lax.scan(advance, start_state, (carry_keep, final_log, fresh_states))
    reach_weight = (
        jnp.exp(running) * (block_seg == prior_seg[:, None]).astype(jnp.float32)[:, :, None]
    )
    carried = jnp.einsum(
        "cih,cin,chpn->cihp", reach_weight, readout_blocks, entering, precision=exact_mode
    )
    outputs = (within + carried).reshape(row_count, head_count, head_width) + head_scalars[2][
        None, :, None
    ] * heads_in
    return outputs.reshape(row_count, head_count * head_width)


def schulz_kernel(
    place, pieces, result, iterate, gram, mixed, low, poly, mixed_low, product, arrived
):
    holders, column_blocks, rows, columns = pieces.shape
    width = iterate.shape[0]
    blocks = width // TILE
    lead, slope, curve = schulz_terms

    def piece_copy(index):
        holder = index // column_blocks
        block = index % column_blocks
        return pltpu.make_async_copy(
            pieces.at[holder, block],
            iterate.at[
                pl.ds(pl.multiple_of(holder * rows, rows), rows),
                pl.ds(pl.multiple_of(block * columns, columns), columns),
            ],
            arrived.at[index],
        )

    def begin(index, carry):
        piece_copy(index).start()
        return carry

    def finish(index, carry):
        piece_copy(index).wait()
        return carry

    lax.fori_loop(0, holders * column_blocks, begin, 0)
    lax.fori_loop(0, holders * column_blocks, finish, 0)
    unit_rows = lax.broadcasted_iota(jnp.int32, (TILE, TILE), 0)
    unit_columns = lax.broadcasted_iota(jnp.int32, (TILE, TILE), 1)
    diagonal = unit_rows == unit_columns
    unit = jnp.where(diagonal, 1.0, 0.0).astype(jnp.bfloat16)

    def band(index):
        return slice(index * TILE, (index + 1) * TILE)

    def tail(index):
        return slice(index * TILE, width)

    def mirror(target):
        for upper in range(blocks):
            for right in range(upper + 1, blocks):
                flipped = lax.dot_general(
                    unit,
                    target[band(upper), band(right)],
                    (((1,), (1,)), ((), ())),
                    preferred_element_type=jnp.float32,
                )
                target[band(right), band(upper)] = flipped.astype(jnp.bfloat16)

    def half_product(left, right, finish_band):
        for index in range(blocks):
            finish_band(
                index,
                jnp.dot(
                    left[band(index), :],
                    right[:, tail(index)],
                    preferred_element_type=jnp.float32,
                ),
            )

    def sweep(step, carry):
        lead_power, shrink = carry
        opening = (step == 0) | (step == GROUP)

        @pl.when(opening)
        def _():
            for index in range(blocks):
                gram[band(index), tail(index)] = lax.dot_general(
                    iterate[band(index), :],
                    iterate[tail(index), :],
                    (((1,), (1,)), ((), ())),
                    preferred_element_type=jnp.float32,
                )

        trace = jnp.float32(0.0)
        for index in range(blocks):
            trace = trace + jnp.sum(jnp.where(diagonal, gram[band(index), band(index)], 0.0))
        shrink = jnp.where(
            step == 0, 1.0 / (jnp.sqrt(jnp.full((1, 1), trace)) + 1e-07), shrink
        )
        square = shrink * shrink

        @pl.when(opening)
        def _():
            scale = jnp.where(step == 0, square, jnp.ones_like(square))
            for index in range(blocks):
                scaled = gram[band(index), tail(index)] * scale
                gram[band(index), tail(index)] = scaled
                low[band(index), tail(index)] = scaled.astype(jnp.bfloat16)
            mirror(low)

        def keep_poly(index, squared):
            poly[band(index), tail(index)] = (
                slope * gram[band(index), tail(index)] + curve * squared
            ).astype(jnp.bfloat16)

        half_product(low, low, keep_poly)
        mirror(poly)
        newest = product.at[step % 2]
        older = product.at[(step + 1) % 2]

        @pl.when(opening)
        def _():
            newest[...] = poly[...]

        @pl.when(jnp.logical_not(opening))
        def _():
            def keep_product(index, multiplied):
                newest[band(index), tail(index)] = (
                    lead * older[band(index), tail(index)].astype(jnp.float32)
                    + lead_power * poly[band(index), tail(index)].astype(jnp.float32)
                    + multiplied
                ).astype(jnp.bfloat16)

            half_product(poly, older, keep_product)
            mirror(newest)

        lead_power = jnp.where(opening, jnp.float32(lead), lead_power * lead)

        @pl.when(step != GROUP - 1)
        def _():
            def keep_mixed(index, multiplied):
                grown = lead * gram[band(index), tail(index)] + multiplied
                mixed[band(index), tail(index)] = grown
                mixed_low[band(index), tail(index)] = grown.astype(jnp.bfloat16)

            half_product(poly, low, keep_mixed)

            @pl.when(step == GROUP)
            def _():
                for index in range(blocks):
                    older[band(index), tail(index)] = (
                        gram[band(index), tail(index)]
                        - low[band(index), tail(index)].astype(jnp.float32)
                    ).astype(jnp.bfloat16)
                mirror(older)

                def add_rest(index, multiplied):
                    grown = mixed[band(index), tail(index)] + multiplied
                    mixed[band(index), tail(index)] = grown
                    mixed_low[band(index), tail(index)] = grown.astype(jnp.bfloat16)

                half_product(poly, older, add_rest)

            mirror(mixed_low)

            def keep_gram(index, multiplied):
                fresh = lead * mixed[band(index), tail(index)] + multiplied
                gram[band(index), tail(index)] = fresh
                low[band(index), tail(index)] = fresh.astype(jnp.bfloat16)

            half_product(poly, mixed_low, keep_gram)
            mirror(low)

        @pl.when(step == GROUP - 1)
        def _():
            def advance(block, carry):
                here = pl.ds(pl.multiple_of(block * SLAB, SLAB), SLAB)
                moved = jnp.dot(newest[...], iterate[:, here], preferred_element_type=jnp.float32)
                iterate[:, here] = (
                    shrink * (lead_power * iterate[:, here].astype(jnp.float32) + moved)
                ).astype(jnp.bfloat16)
                return carry

            lax.fori_loop(0, iterate.shape[1] // SLAB, advance, 0)

        return lead_power, shrink

    lead_power, shrink = lax.fori_loop(
        0, SCHULZ - 1, sweep, (jnp.float32(1.0), jnp.ones((1, 1), jnp.float32))
    )
    last = product.at[(SCHULZ - 2) % 2]
    rest = product.at[(SCHULZ - 1) % 2]
    for index in range(blocks):
        rest[band(index), tail(index)] = (
            gram[band(index), tail(index)] - low[band(index), tail(index)].astype(jnp.float32)
        ).astype(jnp.bfloat16)
    mirror(rest)
    mine = pl.ds(pl.multiple_of(place[0] * rows, rows), rows)
    squared = jnp.dot(low[mine, :], low[...], preferred_element_type=jnp.float32)
    own_gram = low[mine, :].astype(jnp.float32) + rest[mine, :].astype(jnp.float32)
    own_poly = (slope * own_gram + curve * squared).astype(jnp.bfloat16)
    own_product = (
        lead * last[mine, :].astype(jnp.float32)
        + lead_power * own_poly.astype(jnp.float32)
        + jnp.dot(own_poly, last[...], preferred_element_type=jnp.float32)
    )
    own_high = own_product.astype(jnp.bfloat16)
    own_low = (own_product - own_high.astype(jnp.float32)).astype(jnp.bfloat16)
    halves = jnp.concatenate([own_high, own_low], axis=0)
    for block in range(column_blocks):
        here = slice(block * columns, (block + 1) * columns)
        moved = jnp.dot(halves, iterate[:, here], preferred_element_type=jnp.float32)
        result[block] = (
            (lead_power * lead) * iterate[mine, here].astype(jnp.float32)
            + (moved[:rows] + moved[rows:])
        ).astype(jnp.bfloat16)


def own_schulz(pieces, place):
    holders, column_blocks, rows, columns = pieces.shape
    width = holders * rows
    flops = 2 * width * width * (10 * width + 3 * column_blocks * columns)
    return pl.pallas_call(
        schulz_kernel,
        name="schulz",
        out_shape=jax.ShapeDtypeStruct((column_blocks, rows, columns), jnp.bfloat16),
        in_specs=[
            pl.BlockSpec(memory_space=pltpu.SMEM),
            pl.BlockSpec(memory_space=pl.ANY),
        ],
        out_specs=pl.BlockSpec(memory_space=pltpu.VMEM),
        scratch_shapes=[
            pltpu.VMEM((width, column_blocks * columns), jnp.bfloat16),
            pltpu.VMEM((width, width), jnp.float32),
            pltpu.VMEM((width, width), jnp.float32),
            pltpu.VMEM((width, width), jnp.bfloat16),
            pltpu.VMEM((width, width), jnp.bfloat16),
            pltpu.VMEM((width, width), jnp.bfloat16),
            pltpu.VMEM((2, width, width), jnp.bfloat16),
            pltpu.SemaphoreType.DMA((holders * column_blocks,)),
        ],
        compiler_params=pltpu.CompilerParams(vmem_limit_bytes=62 * 1024 * 1024),
        cost_estimate=pl.CostEstimate(
            flops=flops, bytes_accessed=4 * width * columns * column_blocks, transcendentals=0
        ),
    )(place, pieces)


def plain_update(weight, moment, gradient):
    fresh = moment_decay * moment + gradient
    return (weight - plain_rate * fresh, fresh)


def local(
    tokens,
    cotangent,
    lengths,
    gate_weight,
    inner_weight,
    output_weight,
    delta_weight,
    state_weight,
    inner_filter,
    state_filter,
    head_scalars,
    norm_gain,
    input_gain,
    gate_moment,
    inner_moment,
    output_moment,
    delta_moment,
    state_moment,
    inner_filter_moment,
    state_filter_moment,
    head_scalars_moment,
    norm_gain_moment,
    input_gain_moment,
):
    row_count = tokens.shape[0]
    segment, position = packing_layout(lengths[0], row_count)
    columns = gate_weight.shape[1]
    head_count = delta_weight.shape[1]
    mixing_cols = 2 * columns + head_count
    in_rows = jnp.concatenate([gate_weight, inner_weight, delta_weight, state_weight], axis=1)
    in_matrix = lax.all_gather(in_rows.astype(jnp.bfloat16), "dp", axis=0, tiled=True)
    full_output = lax.all_gather(output_weight.astype(jnp.bfloat16), "dp", axis=0, tiled=True)
    full_state = in_matrix[:, mixing_cols:]
    tokens_wide = tokens.astype(jnp.float32)
    root_scale = lax.rsqrt(
        jnp.mean(tokens_wide * tokens_wide, axis=1, keepdims=True) + norm_epsilon
    )
    normed = (tokens_wide * root_scale * input_gain).astype(jnp.bfloat16)
    projected = jnp.dot(normed, in_matrix, preferred_element_type=jnp.float32)
    gate_part = projected[:, :columns]
    inner_part = projected[:, columns : 2 * columns]
    delta_raw = projected[:, 2 * columns : mixing_cols]
    state_raw = projected[:, mixing_cols:]

    def state_rows(raw_values, taps):
        filtered = causal_filter(raw_values, taps, position)
        return (filtered[:, :NSTATE], filtered[:, NSTATE:])

    def mixer(inner_in, delta_in, entry_in, readout_in, taps, scalars):
        return state_mixer(
            inner_in, delta_in, entry_in, readout_in, taps, scalars, segment, position
        )

    (entry_rows, readout_rows), state_back = jax.vjp(state_rows, state_raw, state_filter)
    mixed_rows, mixer_back = jax.vjp(
        mixer,
        inner_part,
        delta_raw,
        entry_rows,
        readout_rows,
        inner_filter,
        head_scalars,
    )
    gate_sigmoid = jax.nn.sigmoid(gate_part)
    gate_silu = gate_part * gate_sigmoid
    gated = mixed_rows * gate_silu
    grad_normalized = jnp.dot(cotangent, full_output, preferred_element_type=jnp.float32)
    weighted = grad_normalized * norm_gain
    squares, inner_dot = lax.psum(
        jnp.stack([jnp.sum(gated * gated, axis=1), jnp.sum(weighted * gated, axis=1)]), "tensor"
    )
    norm_scale = lax.rsqrt(squares / INNER + norm_epsilon)[:, None]
    normalized = (gated * norm_scale * norm_gain).astype(jnp.bfloat16)
    partial_out = jnp.einsum(
        "ti,di->td", normalized, full_output, preferred_element_type=jnp.float32
    )
    output_local = jnp.einsum(
        "td,ti->di", cotangent, normalized, preferred_element_type=jnp.float32
    )
    norm_gain_local = jnp.sum(grad_normalized * gated * norm_scale, axis=0)
    grad_gated = norm_scale * weighted - gated * norm_scale**3 * (inner_dot / INNER)[:, None]
    grad_gate = (
        grad_gated * mixed_rows * (gate_sigmoid + gate_silu * (1.0 - gate_sigmoid))
    ).astype(jnp.bfloat16)

    def weight_gradient(columns_grad):
        return jnp.einsum("td,tk->dk", normed, columns_grad, preferred_element_type=jnp.float32)

    def scattered(partial):
        low = partial.astype(jnp.bfloat16)
        return lax.psum_scatter(low, "dp", scatter_dimension=0, tiled=True)

    output_low, gate_low, grad_mixed = lax.optimization_barrier(
        (
            output_local.astype(jnp.bfloat16),
            weight_gradient(grad_gate).astype(jnp.bfloat16),
            grad_gated * gate_silu,
        )
    )
    output_sum = scattered(output_low)
    gate_sum = scattered(gate_low)
    grad_inner, grad_delta, grad_entry, grad_readout, filter_local, scalar_local = mixer_back(
        grad_mixed
    )
    grad_inner = grad_inner.astype(jnp.bfloat16)
    inner_sum = scattered(weight_gradient(grad_inner))
    entry_total, readout_total = lax.psum((grad_entry, grad_readout), "tensor")
    entry_total, readout_total, _, _, _ = lax.optimization_barrier(
        (entry_total, readout_total, output_sum, gate_sum, inner_sum)
    )
    grad_state, state_filter_local = state_back((entry_total, readout_total))
    grad_delta = grad_delta.astype(jnp.bfloat16)
    grad_mixing = jnp.concatenate([grad_gate, grad_inner, grad_delta], axis=1)
    grad_state_low = grad_state.astype(jnp.bfloat16)
    input_partial = jnp.einsum(
        "tk,dk->td", grad_mixing, in_matrix[:, :mixing_cols], preferred_element_type=jnp.float32
    )
    state_local = jnp.einsum(
        "td,tk->dk", normed, grad_state_low, preferred_element_type=jnp.float32
    )
    state_input = jnp.einsum(
        "tk,dk->td", grad_state_low, full_state, preferred_element_type=jnp.float32
    )
    input_gain_local = jnp.sum(
        (input_partial + state_input / lax.axis_size("tensor")) * tokens_wide * root_scale, axis=0
    )

    output_sum, gate_sum, inner_sum = (
        total.astype(jnp.float32) for total in (output_sum, gate_sum, inner_sum)
    )
    fresh_stack = moment_decay * jnp.stack([gate_moment, inner_moment, output_moment]) + jnp.stack(
        [gate_sum, inner_sum, output_sum]
    )
    spare = jnp.zeros((lax.axis_size("tensor") - 3,) + fresh_stack.shape[1:], jnp.bfloat16)
    rounded_stack = jnp.concatenate([fresh_stack.astype(jnp.bfloat16), spare], axis=0)
    filter_sum, scalar_sum, norm_gain_sum = lax.psum(
        (filter_local, scalar_local, norm_gain_local), "dp"
    )
    rounded_stack, filter_sum, scalar_sum, norm_gain_sum = lax.optimization_barrier(
        (rounded_stack, filter_sum, scalar_sum, norm_gain_sum)
    )
    input_gain_local = lax.psum(input_gain_local, "tensor")
    own_rows = lax.all_to_all(rounded_stack, "tensor", split_axis=0, concat_axis=0, tiled=True)
    whole = lax.all_gather(own_rows, "dp", axis=0)
    side = jnp.concatenate([state_local, weight_gradient(grad_delta)], axis=1)
    whole, out_low, input_low, side, input_gain_local = lax.optimization_barrier(
        (
            whole,
            partial_out.astype(jnp.bfloat16),
            input_partial.astype(jnp.bfloat16),
            side.astype(jnp.bfloat16),
            input_gain_local,
        )
    )
    out_total, input_total = lax.psum((out_low, input_low), "tensor")
    side_sum = lax.psum_scatter(side, "dp", scatter_dimension=0, tiled=True)
    produced = own_schulz(whole, lax.axis_index("dp").reshape(1).astype(jnp.int32))
    (
        out_total,
        input_total,
        side_sum,
        state_filter_local,
        input_gain_local,
        _,
    ) = lax.optimization_barrier(
        (
            out_total,
            input_total,
            side_sum,
            state_filter_local,
            input_gain_local,
            produced[0, :16, :128],
        )
    )
    ortho = lax.all_to_all(produced, "tensor", split_axis=0, concat_axis=0, tiled=True)[:3]
    state_filter_sum, input_gain_sum = lax.psum((state_filter_local, input_gain_local), "dp")
    ortho, state_filter_sum, input_gain_sum = lax.optimization_barrier(
        (ortho, state_filter_sum, input_gain_sum)
    )
    side_sum = side_sum.astype(jnp.float32)
    state_sum = side_sum[:, : 2 * NSTATE]
    delta_sum = side_sum[:, 2 * NSTATE :]
    block_output = (tokens_wide + out_total.astype(jnp.float32)).astype(jnp.bfloat16)
    grad_normed = input_total.astype(jnp.float32) + state_input
    weighted_in = grad_normed * input_gain
    row_mean = jnp.mean(weighted_in * tokens_wide, axis=1, keepdims=True)
    input_gradient = (
        cotangent.astype(jnp.float32)
        + root_scale * weighted_in
        - tokens_wide * root_scale**3 * row_mean
    )
    factor = 0.2 * math.sqrt(max(D, INNER))
    muon_new = jnp.stack(
        [gate_weight, inner_weight, output_weight]
    ) - muon_rate * factor * ortho.astype(jnp.float32)
    delta_updated, delta_moment_new = plain_update(delta_weight, delta_moment, delta_sum)
    state_updated, state_moment_new = plain_update(state_weight, state_moment, state_sum)
    filter_updated, filter_moment_new = plain_update(inner_filter, inner_filter_moment, filter_sum)
    state_filter_updated, state_filter_moment_new = plain_update(
        state_filter, state_filter_moment, state_filter_sum
    )
    scalar_updated, scalar_moment_new = plain_update(head_scalars, head_scalars_moment, scalar_sum)
    norm_gain_updated, norm_gain_moment_new = plain_update(
        norm_gain, norm_gain_moment, norm_gain_sum
    )
    input_gain_updated, input_gain_moment_new = plain_update(
        input_gain, input_gain_moment, input_gain_sum
    )
    return (
        block_output,
        input_gradient,
        gate_sum,
        inner_sum,
        output_sum,
        delta_sum,
        state_sum,
        filter_sum,
        state_filter_sum,
        scalar_sum,
        norm_gain_sum,
        input_gain_sum,
        muon_new[0],
        muon_new[1],
        muon_new[2],
        delta_updated,
        state_updated,
        filter_updated,
        state_filter_updated,
        scalar_updated,
        norm_gain_updated,
        input_gain_updated,
        fresh_stack[0],
        fresh_stack[1],
        fresh_stack[2],
        delta_moment_new,
        state_moment_new,
        filter_moment_new,
        state_filter_moment_new,
        scalar_moment_new,
        norm_gain_moment_new,
        input_gain_moment_new,
    )


def solution(mesh):
    placed = (
        P("dp", None),
        P("dp", None),
        P("dp", None),
        P("dp", "tensor"),
        P("dp", "tensor"),
        P("dp", "tensor"),
        P("dp", "tensor"),
        P("dp", None),
        P(None, "tensor"),
        P(),
        P(None, "tensor"),
        P("tensor"),
        P(),
        P("dp", "tensor"),
        P("dp", "tensor"),
        P("dp", "tensor"),
        P("dp", "tensor"),
        P("dp", None),
        P(None, "tensor"),
        P(),
        P(None, "tensor"),
        P("tensor"),
        P(),
    )
    return jax.shard_map(
        local,
        mesh=mesh,
        in_specs=placed,
        out_specs=(
            P("dp", None),
            P("dp", None),
            P("dp", "tensor"),
            P("dp", "tensor"),
            P("dp", "tensor"),
            P("dp", "tensor"),
            P("dp", None),
            P(None, "tensor"),
            P(),
            P(None, "tensor"),
            P("tensor"),
            P(),
            P("dp", "tensor"),
            P("dp", "tensor"),
            P("dp", "tensor"),
            P("dp", "tensor"),
            P("dp", None),
            P(None, "tensor"),
            P(),
            P(None, "tensor"),
            P("tensor"),
            P(),
            P("dp", "tensor"),
            P("dp", "tensor"),
            P("dp", "tensor"),
            P("dp", "tensor"),
            P("dp", None),
            P(None, "tensor"),
            P(),
            P(None, "tensor"),
            P("tensor"),
            P(),
        ),
        check_vma=False,
    )
```
